32 devices in a mesh: tm: 4 (over y, x), rows: 2 (over core), cols: 4 (over z).
Axes of the slice: x: 2, y: 2, z: 4, core: 2. Of those that a mesh axis runs over, the one named last changes fastest.
Arguments:
- inputs: bfloat16 [4, 34, 32, 128], P('tm', 'rows', 'cols'), may hold values from -6 to 6
- cotangent: bfloat16 [4, 34, 32, 128], P('tm', 'rows', 'cols'), may hold values from -6 to 6
- weight_one: bfloat16 [27, 128, 128], replicated, may hold values from -0.109375 to 0.109375
- weight_two: bfloat16 [27, 128, 128], replicated, may hold values from -0.109375 to 0.109375
Outputs:
- grad_inputs: float32 [4, 34, 32, 128], P('tm', 'rows', 'cols')
- grad_one: float32 [27, 128, 128], P(None, ('tm', 'rows'), 'cols')
- grad_two: float32 [27, 128, 128], P(None, ('tm', 'rows'), 'cols')
The draws below stay inside these ranges and needn't reach their ends.
All inputs are finite; a program needn't handle non-finite values.
Results may differ from the reference program's by a relative error of at most 0.0029.
Values may be sent and summed in bfloat16 or wider, within the bound.
A program may use at most 64 MiB of HBM per device.

```python
import jax
import jax.numpy as jnp

C = 128
FRAMES = 4
HEIGHT = 34
WIDTH = 32


def strengthened(values, key, source, target, shards_of, factor):
    def block_of(dim):
        return (jnp.arange(values.shape[dim]) // (values.shape[dim] // shards_of)).reshape((-1,) + (1,) * (values.ndim - 1 - dim))

    one_side = jax.random.permutation(key, shards_of)[block_of(target)]
    other_side = (block_of(target) + shards_of // 2) % shards_of
    return jnp.where((block_of(source) == one_side) | (block_of(source) == other_side), factor * values, values)


def shard_levels(stream_key, extent, cuts, least, top_value):
    factor_of, own = 1.0, jax.random.fold_in(stream_key, 6)
    for position, parts in cuts:
        draws = jnp.exp(jax.random.uniform(jax.random.fold_in(own, position), (parts,), jnp.float32, least / len(cuts), top_value / len(cuts)))
        factor_of = factor_of * jnp.repeat(draws, extent[position] // parts).reshape([-1 if axis == position else 1 for axis in range(len(extent))])
    return factor_of


def scatter_about(key, extent, deviation, limit, split=(), held_as=jnp.bfloat16):
    level = shard_levels(key, extent, split, -0.22, 0.18) if split else 1.0
    array = jax.random.normal(key, extent, jnp.float32) * deviation * level
    return jnp.minimum(jnp.maximum(array, -limit), limit).astype(held_as)


def bell_draw_with(stream_key, extent, deviation, reach, shards, heavy, kind=jnp.bfloat16):
    drawn = deviation * jax.random.normal(stream_key, extent, jnp.float32)
    if shards:
        drawn = drawn * shard_levels(stream_key, extent, shards, -0.22, 0.18)
    return jnp.clip(strengthened(drawn, jax.random.fold_in(stream_key, 3), *heavy), -reach, reach).astype(kind)


def setup_inputs(seed: int = 0) -> dict:
    keys = jax.random.split(jax.random.key(seed), 5)
    inputs = bell_draw_with(keys[0], (FRAMES, HEIGHT, WIDTH, C), 1.0, 6.0, ((0, 4), (1, 2), (2, 4)), (1, 3, 2, 2.0))
    cotangent = bell_draw_with(keys[1], (FRAMES, HEIGHT, WIDTH, C), 1.0, 6.0, ((0, 4), (1, 2), (2, 4)), (2, 3, 4, 2.0))
    weight_one = scatter_about(keys[2], (27, C, C), (27 * C) ** -0.5, 0.109375)
    weight_two = scatter_about(keys[3], (27, C, C), (27 * C) ** -0.5, 0.109375)
    return dict(inputs=inputs, cotangent=cotangent, weight_one=weight_one, weight_two=weight_two)


def past_pad(volume):
    return jnp.pad(volume, ((2, 0), (1, 1), (1, 1), (0, 0)))

def future_pad(volume):
    return jnp.pad(volume, ((0, 2), (1, 1), (1, 1), (0, 0)))

def convolve(padded, weight, adjoint):
    total = jnp.zeros((FRAMES * HEIGHT * WIDTH, C), jnp.float32)
    for t_off in range(3):
        for h_off in range(3):
            for w_off in range(3):
                tap_index = t_off * 9 + h_off * 3 + w_off
                if adjoint:
                    window = padded[2 - t_off:2 - t_off + FRAMES, 2 - h_off:2 - h_off + HEIGHT, 2 - w_off:2 - w_off + WIDTH]
                    matrix = weight[tap_index].T
                else:
                    window = padded[t_off:t_off + FRAMES, h_off:h_off + HEIGHT, w_off:w_off + WIDTH]
                    matrix = weight[tap_index]
                total = total + jnp.dot(window.reshape(-1, C), matrix, preferred_element_type=jnp.float32)
    return total

def kernel_grad(padded, right_side):
    pieces = []
    for t_off in range(3):
        for h_off in range(3):
            for w_off in range(3):
                window = padded[t_off:t_off + FRAMES, h_off:h_off + HEIGHT, w_off:w_off + WIDTH].reshape(-1, C)
                pieces.append(jnp.dot(window.T, right_side, preferred_element_type=jnp.float32))
    return jnp.stack(pieces)

def reference(inputs, cotangent, weight_one, weight_two):
    hidden = convolve(past_pad(inputs), weight_one, False)
    squash = jax.nn.sigmoid(hidden)
    activation = (hidden * squash).astype(jnp.bfloat16)
    flat_grad = cotangent.reshape(-1, C)
    grad_act = convolve(future_pad(cotangent), weight_two, True)
    grad_hidden = (grad_act * squash * (1.0 + hidden * (1.0 - squash))).astype(jnp.bfloat16)
    grad_two = kernel_grad(past_pad(activation.reshape(FRAMES, HEIGHT, WIDTH, C)), flat_grad)
    grad_one = kernel_grad(past_pad(inputs), grad_hidden)
    back = convolve(future_pad(grad_hidden.reshape(FRAMES, HEIGHT, WIDTH, C)), weight_one, True)
    grad_inputs = cotangent.astype(jnp.float32) + back.reshape(FRAMES, HEIGHT, WIDTH, C)
    return (grad_inputs, grad_one, grad_two)
```

```python
import functools

import jax
import jax.numpy as jnp
from jax import lax
from jax.experimental import pallas as pl
from jax.experimental.pallas import tpu as pltpu
from jax.sharding import PartitionSpec as P

MESH = pl.DeviceIdType.MESH
NT = (((1,), (1,)), ((), ()))


def kernel(
    dims,
    block_ref,
    edge_ref,
    w1_ref,
    w2_ref,
    back_ref,
    one_ref,
    two_ref,
    gat,
    left,
    right,
    sx,
    sg,
    sh,
    sa,
    imc,
    w1r,
    w2r,
    lt,
    pp,
    edges_out,
    edges_in,
    stage,
    landed,
    acc,
    own_sem,
    blk_send,
    blk_recv,
    low_send,
    low_recv,
    high_send,
    high_recv,
    gh_send,
    gh_recv,
    rs_send,
    rs_recv,
):
    tmn, rn, zn, rows, cols, chunk, chunk_pad, slots = dims
    plane = tmn * rn
    height = rn * rows
    pitch = (height + 2) * cols
    cells = rows * cols
    frame_cells = height * cols
    span = tmn * pitch
    ochunk = 128 // zn
    tm, row, col = lax.axis_index("tm"), lax.axis_index("rows"), lax.axis_index("cols")
    me = tm * rn + row

    def place(index, z):
        return (index // rn, lax.rem(index, rn), z)

    has_low, has_high = col > 0, col < zn - 1

    barrier = pltpu.get_barrier_semaphore()

    def greet(index, z):
        pl.semaphore_signal(barrier, inc=1, device_id=place(index, z), device_id_type=MESH)

    for d in range(1, plane):
        greet(lax.rem(me + d, plane), col)

    @pl.when(has_low)
    def _():
        for d in range(plane):
            greet(lax.rem(me + d, plane), col - 1)

    @pl.when(has_high)
    def _():
        for d in range(plane):
            greet(lax.rem(me + d, plane), col + 1)

    for z in range(zn):

        @pl.when((z > col + 1) | (z < col - 1))
        def _():
            greet(me, z)

    own = pltpu.make_async_copy(block_ref, gat.at[me], own_sem)
    own.start()

    for k in range(27):
        w1r[:, 128 * k : 128 * (k + 1)] = w1_ref[128 * k : 128 * (k + 1), :]
        w2r[:, 128 * k : 128 * (k + 1)] = w2_ref[128 * k : 128 * (k + 1), :]
    for buffer in (sx, sg, sh):
        buffer[...] = jnp.zeros(buffer.shape, buffer.dtype)
    sa[...] = jnp.zeros(sa.shape, sa.dtype)
    lt[...] = jnp.zeros(lt.shape, lt.dtype)
    pp[...] = jnp.zeros(pp.shape, pp.dtype)

    beside = jnp.minimum(col, 1) + jnp.minimum(zn - 1 - col, 1)
    pl.semaphore_wait(barrier, plane - 1 + plane * beside + zn - 1 - beside)

    def send_block(d):
        peer = lax.rem(me + d, plane)
        return pltpu.make_async_remote_copy(
            src_ref=block_ref,
            dst_ref=gat.at[me],
            send_sem=blk_send.at[d],
            recv_sem=blk_recv.at[me],
            device_id=place(peer, col),
            device_id_type=MESH,
        )

    def send_low(d):
        return pltpu.make_async_remote_copy(
            src_ref=edge_ref.at[0],
            dst_ref=right.at[me],
            send_sem=low_send.at[d],
            recv_sem=low_recv.at[me],
            device_id=place(lax.rem(me + d, plane), col - 1),
            device_id_type=MESH,
        )

    def send_high(d):
        return pltpu.make_async_remote_copy(
            src_ref=edge_ref.at[1],
            dst_ref=left.at[me],
            send_sem=high_send.at[d],
            recv_sem=high_recv.at[me],
            device_id=place(lax.rem(me + d, plane), col + 1),
            device_id_type=MESH,
        )

    @pl.when(has_low)
    def _():
        for d in range(plane):
            send_low(d).start()

    @pl.when(has_high)
    def _():
        for d in range(plane):
            send_high(d).start()

    for d in range(1, plane):
        send_block(d).start()
    own.wait()

    def arrived(dst, sem, z):
        pltpu.make_async_remote_copy(
            src_ref=dst, dst_ref=dst, send_sem=sem, recv_sem=sem,
            device_id=place(me, z), device_id_type=MESH,
        ).wait_recv()

    for m in range(plane):
        t, r = m // rn, m % rn

        @pl.when(me != m)
        def _():
            arrived(gat.at[m], blk_recv.at[m], col)

        for which, (dst, frame) in enumerate(((sx, t + 2), (sg, t))):
            base = frame * pitch + (r * rows + 1) * cols
            v = gat[m, which].astype(jnp.float32)
            dst[1, base : base + cells] = v
            dst[0, base + 1 : base + cells] = v[: cells - 1]
            dst[2, base : base + cells - 1] = v[1:]
            nothing = jnp.zeros((rows, 128), jnp.float32)
            dst[0, pl.ds(base, rows, stride=cols), :] = nothing
            dst[2, pl.ds(base + cols - 1, rows, stride=cols), :] = nothing

    @pl.when(has_low)
    def _():
        for m in range(plane):
            arrived(left.at[m], high_recv.at[m], col - 1)
            for which, (dst, frame) in enumerate(((sx, m // rn + 2), (sg, m // rn))):
                base = frame * pitch + (m % rn * rows + 1) * cols
                dst[0, pl.ds(base, rows, stride=cols), :] = left[m, which].astype(jnp.float32)

    @pl.when(has_high)
    def _():
        for m in range(plane):
            arrived(right.at[m], low_recv.at[m], col + 1)
            for which, (dst, frame) in enumerate(((sx, m // rn + 2), (sg, m // rn))):
                base = frame * pitch + (m % rn * rows + 1) * cols + cols - 1
                dst[2, pl.ds(base, rows, stride=cols), :] = right[m, which].astype(jnp.float32)

    def past(src, base, count):
        for k in range(27):
            a, b, e = k // 9, k // 3 % 3, k % 3
            at = pl.multiple_of(base + a * pitch + b * cols, 8)
            imc[:count, 128 * k : 128 * (k + 1)] = src[e, pl.ds(at, count), :].astype(jnp.bfloat16)

    def future(src, base, count):
        for k in range(27):
            a, b, e = k // 9, k // 3 % 3, k % 3
            at = pl.multiple_of(base + (2 - a) * pitch + (2 - b) * cols, 8)
            imc[:count, 128 * k : 128 * (k + 1)] = src[2 - e, pl.ds(at, count), :].astype(jnp.bfloat16)

    def frame_step(t, carry):
        base = pl.multiple_of(t * pitch, 8)
        past(sx, base, frame_cells)
        hidden = jnp.dot(imc[:frame_cells, :], w1_ref[...], preferred_element_type=jnp.float32)
        future(sg, base, frame_cells)
        grad_act = lax.dot_general(
            imc[:frame_cells, :], w2r[...], NT, preferred_element_type=jnp.float32
        )
        squash = jax.nn.sigmoid(hidden)
        activation = (hidden * squash).astype(jnp.bfloat16)
        grad_hidden = (grad_act * squash * (1.0 + hidden * (1.0 - squash))).astype(jnp.bfloat16)
        at = pl.multiple_of(base + cols, 8)
        sa[pl.ds(pl.multiple_of(at + 2 * pitch, 8), frame_cells), :] = activation.astype(jnp.float32)
        sh[1, pl.ds(at, frame_cells), :] = grad_hidden.astype(jnp.float32)
        return carry

    lax.fori_loop(0, tmn, frame_step, 0)

    lines = tmn * (height + 2)
    edges_out[0] = sh[1, pl.ds(0, lines, stride=cols), :].astype(jnp.bfloat16)
    edges_out[1] = sh[1, pl.ds(cols - 1, lines, stride=cols), :].astype(jnp.bfloat16)

    def send_edge(side):
        return pltpu.make_async_remote_copy(
            src_ref=edges_out.at[side],
            dst_ref=edges_in.at[1 - side],
            send_sem=gh_send.at[side],
            recv_sem=gh_recv.at[1 - side],
            device_id=place(me, col - 1 if side == 0 else col + 1),
            device_id_type=MESH,
        )

    @pl.when(has_low)
    def _():
        send_edge(0).start()

    @pl.when(has_high)
    def _():
        send_edge(1).start()

    picked = jnp.where(
        (lax.broadcasted_iota(jnp.int32, (chunk_pad, 128), 1)
         == me * chunk + lax.broadcasted_iota(jnp.int32, (chunk_pad, 128), 0))
        & (lax.broadcasted_iota(jnp.int32, (chunk_pad, 128), 0) < chunk),
        1.0, 0.0,
    ).astype(jnp.bfloat16)

    def tall(src):
        return lax.dot_general(picked, src.astype(jnp.bfloat16), NT, preferred_element_type=jnp.float32)

    group = slots * chunk_pad // zn

    def packed(tensor):
        for z in range(zn):
            stage[z, tensor] = jnp.concatenate(
                [pp[group * q : group * (q + 1), ochunk * z : ochunk * (z + 1)] for q in range(zn)],
                axis=1,
            ).astype(jnp.bfloat16)

    for e in range(3):
        xt = tall(sx[e])
        for ab in range(9):
            off = ab // 3 * pitch + ab % 3 * cols
            k = 3 * ab + e
            lt[k * chunk_pad : (k + 1) * chunk_pad, :] = xt[:, off : off + span].astype(jnp.bfloat16)
    taps = 27 * chunk_pad
    pp[:taps, :] = jnp.dot(
        lt[:taps, :], sh[1, cols : cols + span, :].astype(jnp.bfloat16),
        preferred_element_type=jnp.float32,
    )
    packed(0)
    at = tall(sa[...])
    for ab in range(9):
        off = ab // 3 * pitch + ab % 3 * cols
        lt[ab * chunk_pad : (ab + 1) * chunk_pad, :] = at[:, off : off + span].astype(jnp.bfloat16)
    for e in range(3):
        part = jnp.dot(
            lt[: 9 * chunk_pad, :], sg[2 - e, cols : cols + span, :].astype(jnp.bfloat16),
            preferred_element_type=jnp.float32,
        )
        for ab in range(9):
            k = 3 * ab + e
            pp[k * chunk_pad : (k + 1) * chunk_pad, :] = part[ab * chunk_pad : (ab + 1) * chunk_pad]
    packed(1)

    def send_piece(z):
        return pltpu.make_async_remote_copy(
            src_ref=stage.at[z],
            dst_ref=landed.at[col],
            send_sem=rs_send.at[z],
            recv_sem=rs_recv.at[col],
            device_id=place(me, z),
            device_id_type=MESH,
        )

    for z in range(zn):

        @pl.when(col != z)
        def _():
            send_piece(z).start()

    sh[0, 1 : span, :] = sh[1, : span - 1, :]
    sh[2, : span - 1, :] = sh[1, 1:span, :]
    nothing = jnp.zeros((lines, 128), jnp.float32)
    sh[0, pl.ds(0, lines, stride=cols), :] = nothing
    sh[2, pl.ds(cols - 1, lines, stride=cols), :] = nothing

    @pl.when(has_low)
    def _():
        arrived(edges_in.at[0], gh_recv.at[0], col - 1)
        sh[0, pl.ds(0, lines, stride=cols), :] = edges_in[0].astype(jnp.float32)

    @pl.when(has_high)
    def _():
        arrived(edges_in.at[1], gh_recv.at[1], col + 1)
        sh[2, pl.ds(cols - 1, lines, stride=cols), :] = edges_in[1].astype(jnp.float32)

    future(sh, pl.multiple_of(tm * pitch + row * cells, 8), cells)
    back_ref[...] = block_ref[1].astype(jnp.float32) + lax.dot_general(
        imc[:cells, :], w1r[...], NT, preferred_element_type=jnp.float32
    )

    acc[...] = stage[col].astype(jnp.float32)
    for z in range(zn):

        @pl.when(col != z)
        def _():
            arrived(landed.at[z], rs_recv.at[z], z)
            acc[...] += landed[z].astype(jnp.float32)

    for tensor, out in enumerate((one_ref, two_ref)):
        got = acc[tensor]
        whole = jnp.concatenate(
            [got[:, ochunk * q : ochunk * (q + 1)] for q in range(zn)], axis=0
        ).reshape(slots, chunk_pad, ochunk)
        out[...] = whole[:27, :chunk, :]

    for d in range(1, plane):
        send_block(d).wait_send()

    @pl.when(has_low)
    def _():
        for d in range(plane):
            send_low(d).wait_send()
        send_edge(0).wait_send()

    @pl.when(has_high)
    def _():
        for d in range(plane):
            send_high(d).wait_send()
        send_edge(1).wait_send()

    for z in range(zn):

        @pl.when(col != z)
        def _():
            send_piece(z).wait_send()


def body(sizes, inputs, cotangent, weight_one, weight_two):
    tmn, rn, zn = sizes
    _, rows, cols, channels = inputs.shape
    plane = tmn * rn
    cells = rows * cols
    chunk = channels // plane
    chunk_pad = max(16, chunk)
    slots = 28
    pitch = (rn * rows + 2) * cols
    total = -(-((tmn + 2) * pitch + 2 * cols) // 128) * 128
    both = jnp.concatenate([inputs, cotangent], axis=0)
    blocks = both.reshape(2, cells, channels)
    edges = jnp.stack([both[:, :, 0], both[:, :, cols - 1]])
    dims = (tmn, rn, zn, rows, cols, chunk, chunk_pad, slots)
    vmem = pl.BlockSpec(memory_space=pltpu.VMEM)
    bf, f32 = jnp.bfloat16, jnp.float32
    group = slots * chunk_pad // zn
    lines = tmn * (rn * rows + 2)
    frame_cells = rn * rows * cols
    dma = pltpu.SemaphoreType.DMA
    back, one, two = pl.pallas_call(
        functools.partial(kernel, dims),
        out_shape=(
            jax.ShapeDtypeStruct((cells, channels), f32),
            jax.ShapeDtypeStruct((27, chunk, channels // zn), f32),
            jax.ShapeDtypeStruct((27, chunk, channels // zn), f32),
        ),
        in_specs=[vmem] * 4,
        out_specs=(vmem,) * 3,
        scratch_shapes=[
            pltpu.VMEM((plane, 2, cells, channels), bf),
            pltpu.VMEM((plane, 2, rows, channels), bf),
            pltpu.VMEM((plane, 2, rows, channels), bf),
            pltpu.VMEM((3, total, channels), f32),
            pltpu.VMEM((3, total, channels), f32),
            pltpu.VMEM((3, total, channels), f32),
            pltpu.VMEM((total, channels), f32),
            pltpu.VMEM((frame_cells, 27 * channels), bf),
            pltpu.VMEM((channels, 27 * channels), bf),
            pltpu.VMEM((channels, 27 * channels), bf),
            pltpu.VMEM((slots * chunk_pad, tmn * pitch), bf),
            pltpu.VMEM((slots * chunk_pad, channels), f32),
            pltpu.VMEM((2, lines, channels), bf),
            pltpu.VMEM((2, lines, channels), bf),
            pltpu.VMEM((zn, 2, group, channels), bf),
            pltpu.VMEM((zn, 2, group, channels), bf),
            pltpu.VMEM((2, group, channels), f32),
            dma,
            dma((plane,)),
            dma((plane,)),
            dma((plane,)),
            dma((plane,)),
            dma((plane,)),
            dma((plane,)),
            dma((2,)),
            dma((2,)),
            dma((zn,)),
            dma((zn,)),
        ],
        compiler_params=pltpu.CompilerParams(
            collective_id=0, has_side_effects=True, vmem_limit_bytes=60 * 1024 * 1024
        ),
    )(blocks, edges, weight_one.reshape(27 * channels, channels), weight_two.reshape(27 * channels, channels))
    return back.reshape(1, rows, cols, channels), one, two


def solution(mesh):
    sizes = (mesh.shape["tm"], mesh.shape["rows"], mesh.shape["cols"])
    placed = (P("tm", "rows", "cols", None), P("tm", "rows", "cols", None), P(), P())
    return jax.shard_map(
        functools.partial(body, sizes),
        mesh=mesh,
        in_specs=placed,
        out_specs=(
            P("tm", "rows", "cols", None),
            P(None, ("tm", "rows"), "cols"),
            P(None, ("tm", "rows"), "cols"),
        ),
        check_vma=False,
    )
```

```python
import functools

import jax
import jax.numpy as jnp
from jax import lax
from jax.experimental import pallas as pl
from jax.experimental.pallas import tpu as pltpu
from jax.sharding import PartitionSpec as P

MESH = pl.DeviceIdType.MESH
NT = (((1,), (1,)), ((), ()))


def kernel(
    dims,
    x_ref,
    c_ref,
    w1_ref,
    w2_ref,
    back_ref,
    acc,
    flat,
    edge,
    w1v,
    hid,
    gat,
    left,
    right,
    sx,
    sg,
    sh,
    sa,
    imc,
    w1r,
    w2r,
    lt,
    pp,
    edges_out,
    edges_in,
    stage,
    landed,
    own_sem,
    w1_sem,
    w2_sem,
    blk_send,
    blk_recv,
    low_send,
    low_recv,
    high_send,
    high_recv,
    gh_send,
    gh_recv,
    rs_send,
    rs_recv,
):
    tmn, rn, zn, rows, cols, chunk, chunk_pad, slots = dims
    plane = tmn * rn
    height = rn * rows
    pitch = (height + 2) * cols
    cells = rows * cols
    frame_cells = height * cols
    span = tmn * pitch
    ochunk = 128 // zn
    tm, row, col = lax.axis_index("tm"), lax.axis_index("rows"), lax.axis_index("cols")
    me = tm * rn + row

    def place(index, z):
        return (index // rn, lax.rem(index, rn), z)

    has_low, has_high = col > 0, col < zn - 1

    barrier = pltpu.get_barrier_semaphore()

    def greet(index, z):
        pl.semaphore_signal(barrier, inc=1, device_id=place(index, z), device_id_type=MESH)

    for d in range(1, plane):
        greet(lax.rem(me + d, plane), col)

    @pl.when(has_low)
    def _():
        for d in range(plane):
            greet(lax.rem(me + d, plane), col - 1)

    @pl.when(has_high)
    def _():
        for d in range(plane):
            greet(lax.rem(me + d, plane), col + 1)

    for z in range(zn):

        @pl.when((z > col + 1) | (z < col - 1))
        def _():
            greet(me, z)

    blocks = (x_ref, c_ref)

    def keep(which):
        return pltpu.make_async_copy(blocks[which], gat.at[which, me], own_sem.at[which])

    def load_two(k):
        part = pl.ds(128 * k, 128)
        return pltpu.make_async_copy(w2_ref.at[part, :], w2r.at[:, part], w2_sem.at[k])

    load_one = pltpu.make_async_copy(w1_ref, w1v, w1_sem)
    keep(0).start()
    keep(1).start()
    load_one.start()
    for k in range(27):
        load_two(k).start()

    for which in range(2):
        flat[...] = blocks[which][...].astype(jnp.float32)
        for side in range(2):
            edge[which, side] = flat[pl.ds(side * (cols - 1), rows, stride=cols), :].astype(jnp.bfloat16)
    for buffer in (sx, sg):
        buffer[...] = jnp.zeros(buffer.shape, buffer.dtype)

    beside = jnp.minimum(col, 1) + jnp.minimum(zn - 1 - col, 1)
    pl.semaphore_wait(barrier, plane - 1 + plane * beside + zn - 1 - beside)

    def send_block(which, d):
        peer = lax.rem(me + d, plane)
        return pltpu.make_async_remote_copy(
            src_ref=blocks[which],
            dst_ref=gat.at[which, me],
            send_sem=blk_send.at[which, d],
            recv_sem=blk_recv.at[which, me],
            device_id=place(peer, col),
            device_id_type=MESH,
        )

    def send_low(which, d):
        return pltpu.make_async_remote_copy(
            src_ref=edge.at[which, 0],
            dst_ref=right.at[which, me],
            send_sem=low_send.at[which, d],
            recv_sem=low_recv.at[which, me],
            device_id=place(lax.rem(me + d, plane), col - 1),
            device_id_type=MESH,
        )

    def send_high(which, d):
        return pltpu.make_async_remote_copy(
            src_ref=edge.at[which, 1],
            dst_ref=left.at[which, me],
            send_sem=high_send.at[which, d],
            recv_sem=high_recv.at[which, me],
            device_id=place(lax.rem(me + d, plane), col + 1),
            device_id_type=MESH,
        )

    for which in range(2):
        for d in range(1, plane):
            send_block(which, d).start()

        @pl.when(has_low)
        def _():
            for d in range(plane):
                send_low(which, d).start()

        @pl.when(has_high)
        def _():
            for d in range(plane):
                send_high(which, d).start()

    for buffer in (sh, sa, lt, pp):
        buffer[...] = jnp.zeros(buffer.shape, buffer.dtype)
    load_one.wait()
    for k in range(27):
        w1r[:, 128 * k : 128 * (k + 1)] = w1v[128 * k : 128 * (k + 1), :]
    keep(0).wait()
    keep(1).wait()

    def arrived(dst, sem, z):
        pltpu.make_async_remote_copy(
            src_ref=dst, dst_ref=dst, send_sem=sem, recv_sem=sem,
            device_id=place(me, z), device_id_type=MESH,
        ).wait_recv()

    def gather(which, dst, ahead):
        for m in range(plane):

            @pl.when(me != m)
            def _():
                arrived(gat.at[which, m], blk_recv.at[which, m], col)

            base = (m // rn + ahead) * pitch + (m % rn * rows + 1) * cols
            v = gat[which, m].astype(jnp.float32)
            dst[1, base : base + cells] = v
            dst[0, base + 1 : base + cells] = v[: cells - 1]
            dst[2, base : base + cells - 1] = v[1:]
            nothing = jnp.zeros((rows, 128), jnp.float32)
            dst[0, pl.ds(base, rows, stride=cols), :] = nothing
            dst[2, pl.ds(base + cols - 1, rows, stride=cols), :] = nothing

        @pl.when(has_low)
        def _():
            for m in range(plane):
                arrived(left.at[which, m], high_recv.at[which, m], col - 1)
                base = (m // rn + ahead) * pitch + (m % rn * rows + 1) * cols
                dst[0, pl.ds(base, rows, stride=cols), :] = left[which, m].astype(jnp.float32)

        @pl.when(has_high)
        def _():
            for m in range(plane):
                arrived(right.at[which, m], low_recv.at[which, m], col + 1)
                base = (m // rn + ahead) * pitch + (m % rn * rows + 2) * cols - 1
                dst[2, pl.ds(base, rows, stride=cols), :] = right[which, m].astype(jnp.float32)

    def past(src, base, count):
        for k in range(27):
            a, b, e = k // 9, k // 3 % 3, k % 3
            at = pl.multiple_of(base + a * pitch + b * cols, 8)
            imc[:count, 128 * k : 128 * (k + 1)] = src[e, pl.ds(at, count), :].astype(jnp.bfloat16)

    def future(src, base, count):
        for k in range(27):
            a, b, e = k // 9, k // 3 % 3, k % 3
            at = pl.multiple_of(base + (2 - a) * pitch + (2 - b) * cols, 8)
            imc[:count, 128 * k : 128 * (k + 1)] = src[2 - e, pl.ds(at, count), :].astype(jnp.bfloat16)

    group = slots * chunk_pad // zn
    taps = 27 * chunk_pad
    picked = jnp.where(
        (lax.broadcasted_iota(jnp.int32, (chunk_pad, 128), 1)
         == me * chunk + lax.broadcasted_iota(jnp.int32, (chunk_pad, 128), 0))
        & (lax.broadcasted_iota(jnp.int32, (chunk_pad, 128), 0) < chunk),
        1.0, 0.0,
    ).astype(jnp.bfloat16)

    def tall(src):
        return lax.dot_general(picked, src.astype(jnp.bfloat16), NT, preferred_element_type=jnp.float32)

    def send_piece(tensor, z):
        return pltpu.make_async_remote_copy(
            src_ref=stage.at[tensor, z],
            dst_ref=landed.at[tensor, col],
            send_sem=rs_send.at[tensor, z],
            recv_sem=rs_recv.at[tensor, col],
            device_id=place(me, z),
            device_id_type=MESH,
        )

    def scatter(tensor):
        for z in range(zn):
            stage[tensor, z] = jnp.concatenate(
                [pp[group * q : group * (q + 1), ochunk * z : ochunk * (z + 1)] for q in range(zn)],
                axis=1,
            ).astype(jnp.bfloat16)
        for z in range(zn):

            @pl.when(col != z)
            def _():
                send_piece(tensor, z).start()

    gather(0, sx, 2)

    def forward_step(t, carry):
        base = pl.multiple_of(t * pitch, 8)
        past(sx, base, frame_cells)
        hidden = jnp.dot(imc[:frame_cells, :], w1v[...], preferred_element_type=jnp.float32)
        hid[t] = hidden
        activation = (hidden * jax.nn.sigmoid(hidden)).astype(jnp.bfloat16)
        at = pl.multiple_of(base + cols + 2 * pitch, 8)
        sa[pl.ds(at, frame_cells), :] = activation.astype(jnp.float32)
        return carry

    lax.fori_loop(0, tmn, forward_step, 0)

    gather(1, sg, 0)
    at = tall(sa[...])
    for ab in range(9):
        off = ab // 3 * pitch + ab % 3 * cols
        lt[ab * chunk_pad : (ab + 1) * chunk_pad, :] = at[:, off : off + span].astype(jnp.bfloat16)
    for e in range(3):
        part = jnp.dot(
            lt[: 9 * chunk_pad, :], sg[2 - e, cols : cols + span, :].astype(jnp.bfloat16),
            preferred_element_type=jnp.float32,
        )
        for ab in range(9):
            k = 3 * ab + e
            pp[k * chunk_pad : (k + 1) * chunk_pad, :] = part[ab * chunk_pad : (ab + 1) * chunk_pad]
    scatter(1)

    for k in range(27):
        load_two(k).wait()

    def backward_step(t, carry):
        base = pl.multiple_of(t * pitch, 8)
        future(sg, base, frame_cells)
        grad_act = lax.dot_general(
            imc[:frame_cells, :], w2r[...], NT, preferred_element_type=jnp.float32
        )
        hidden = hid[t]
        squash = jax.nn.sigmoid(hidden)
        grad_hidden = (grad_act * squash * (1.0 + hidden * (1.0 - squash))).astype(jnp.bfloat16)
        at = pl.multiple_of(base + cols, 8)
        sh[1, pl.ds(at, frame_cells), :] = grad_hidden.astype(jnp.float32)
        return carry

    lax.fori_loop(0, tmn, backward_step, 0)

    lines = tmn * (height + 2)
    edges_out[0] = sh[1, pl.ds(0, lines, stride=cols), :].astype(jnp.bfloat16)
    edges_out[1] = sh[1, pl.ds(cols - 1, lines, stride=cols), :].astype(jnp.bfloat16)

    def send_edge(side):
        return pltpu.make_async_remote_copy(
            src_ref=edges_out.at[side],
            dst_ref=edges_in.at[1 - side],
            send_sem=gh_send.at[side],
            recv_sem=gh_recv.at[1 - side],
            device_id=place(me, col - 1 if side == 0 else col + 1),
            device_id_type=MESH,
        )

    @pl.when(has_low)
    def _():
        send_edge(0).start()

    @pl.when(has_high)
    def _():
        send_edge(1).start()

    for e in range(3):
        xt = tall(sx[e])
        for ab in range(9):
            off = ab // 3 * pitch + ab % 3 * cols
            k = 3 * ab + e
            lt[k * chunk_pad : (k + 1) * chunk_pad, :] = xt[:, off : off + span].astype(jnp.bfloat16)
    pp[:taps, :] = jnp.dot(
        lt[:taps, :], sh[1, cols : cols + span, :].astype(jnp.bfloat16),
        preferred_element_type=jnp.float32,
    )
    scatter(0)

    sh[0, 1 : span, :] = sh[1, : span - 1, :]
    sh[2, : span - 1, :] = sh[1, 1:span, :]
    nothing = jnp.zeros((lines, 128), jnp.float32)
    sh[0, pl.ds(0, lines, stride=cols), :] = nothing
    sh[2, pl.ds(cols - 1, lines, stride=cols), :] = nothing

    @pl.when(has_low)
    def _():
        arrived(edges_in.at[0], gh_recv.at[0], col - 1)
        sh[0, pl.ds(0, lines, stride=cols), :] = edges_in[0].astype(jnp.float32)

    @pl.when(has_high)
    def _():
        arrived(edges_in.at[1], gh_recv.at[1], col + 1)
        sh[2, pl.ds(cols - 1, lines, stride=cols), :] = edges_in[1].astype(jnp.float32)

    future(sh, pl.multiple_of(tm * pitch + row * cells, 8), cells)
    back_ref[...] = c_ref[...].astype(jnp.float32) + lax.dot_general(
        imc[:cells, :], w1r[...], NT, preferred_element_type=jnp.float32
    )

    for tensor in (1, 0):
        acc[tensor] = stage[tensor, col].astype(jnp.float32)
        for z in range(zn):

            @pl.when(col != z)
            def _():
                arrived(landed.at[tensor, z], rs_recv.at[tensor, z], z)
                acc[tensor] += landed[tensor, z].astype(jnp.float32)

    for which in range(2):
        for d in range(1, plane):
            send_block(which, d).wait_send()

        @pl.when(has_low)
        def _():
            for d in range(plane):
                send_low(which, d).wait_send()

        @pl.when(has_high)
        def _():
            for d in range(plane):
                send_high(which, d).wait_send()

        for z in range(zn):

            @pl.when(col != z)
            def _():
                send_piece(which, z).wait_send()

    @pl.when(has_low)
    def _():
        send_edge(0).wait_send()

    @pl.when(has_high)
    def _():
        send_edge(1).wait_send()


def finish(zn, chunk, chunk_pad, slots, back_ref, acc_ref, out_ref, one_ref, two_ref):
    ochunk = 128 // zn
    out_ref[...] = back_ref[...]
    for tensor, out in enumerate((one_ref, two_ref)):
        got = acc_ref[tensor]
        whole = jnp.concatenate(
            [got[:, ochunk * q : ochunk * (q + 1)] for q in range(zn)], axis=0
        ).reshape(slots, chunk_pad, ochunk)
        out[...] = whole[:27, :chunk, :]


def body(sizes, inputs, cotangent, weight_one, weight_two):
    tmn, rn, zn = sizes
    _, rows, cols, channels = inputs.shape
    plane = tmn * rn
    cells = rows * cols
    chunk = channels // plane
    chunk_pad = max(16, chunk)
    slots = 28
    pitch = (rn * rows + 2) * cols
    total = -(-((tmn + 2) * pitch + 2 * cols) // 128) * 128
    dims = (tmn, rn, zn, rows, cols, chunk, chunk_pad, slots)
    vmem = pl.BlockSpec(memory_space=pltpu.VMEM)
    bf, f32 = jnp.bfloat16, jnp.float32
    group = slots * chunk_pad // zn
    lines = tmn * (rn * rows + 2)
    frame_cells = rn * rows * cols
    dma = pltpu.SemaphoreType.DMA
    back, acc = pl.pallas_call(
        functools.partial(kernel, dims),
        out_shape=(
            jax.ShapeDtypeStruct((cells, channels), f32),
            jax.ShapeDtypeStruct((2, group, channels), f32),
        ),
        in_specs=[vmem] * 2 + [pl.BlockSpec(memory_space=pl.ANY)] * 2,
        out_specs=(vmem,) * 2,
        scratch_shapes=[
            pltpu.VMEM((cells, channels), f32),
            pltpu.VMEM((2, 2, rows, channels), bf),
            pltpu.VMEM((27 * channels, channels), bf),
            pltpu.VMEM((tmn, frame_cells, channels), f32),
            pltpu.VMEM((2, plane, cells, channels), bf),
            pltpu.VMEM((2, plane, rows, channels), bf),
            pltpu.VMEM((2, plane, rows, channels), bf),
            pltpu.VMEM((3, total, channels), f32),
            pltpu.VMEM((3, total, channels), f32),
            pltpu.VMEM((3, total, channels), f32),
            pltpu.VMEM((total, channels), f32),
            pltpu.VMEM((frame_cells, 27 * channels), bf),
            pltpu.VMEM((channels, 27 * channels), bf),
            pltpu.VMEM((channels, 27 * channels), bf),
            pltpu.VMEM((slots * chunk_pad, tmn * pitch), bf),
            pltpu.VMEM((slots * chunk_pad, channels), f32),
            pltpu.VMEM((2, lines, channels), bf),
            pltpu.VMEM((2, lines, channels), bf),
            pltpu.VMEM((2, zn, group, channels), bf),
            pltpu.VMEM((2, zn, group, channels), bf),
            dma((2,)),
            dma,
            dma((27,)),
            dma((2, plane)),
            dma((2, plane)),
            dma((2, plane)),
            dma((2, plane)),
            dma((2, plane)),
            dma((2, plane)),
            dma((2,)),
            dma((2,)),
            dma((2, zn)),
            dma((2, zn)),
        ],
        compiler_params=pltpu.CompilerParams(
            collective_id=0, has_side_effects=True, vmem_limit_bytes=60 * 1024 * 1024
        ),
    )(
        inputs.reshape(cells, channels),
        cotangent.reshape(cells, channels),
        weight_one.reshape(27 * channels, channels),
        weight_two.reshape(27 * channels, channels),
    )
    back, one, two = pl.pallas_call(
        functools.partial(finish, zn, chunk, chunk_pad, slots),
        out_shape=(
            jax.ShapeDtypeStruct((cells, channels), f32),
            jax.ShapeDtypeStruct((27, chunk, channels // zn), f32),
            jax.ShapeDtypeStruct((27, chunk, channels // zn), f32),
        ),
        in_specs=[vmem] * 2,
        out_specs=(vmem,) * 3,
    )(back, acc)
    return back.reshape(1, rows, cols, channels), one, two


def solution(mesh):
    sizes = (mesh.shape["tm"], mesh.shape["rows"], mesh.shape["cols"])
    placed = (P("tm", "rows", "cols", None), P("tm", "rows", "cols", None), P(), P())
    return jax.shard_map(
        functools.partial(body, sizes),
        mesh=mesh,
        in_specs=placed,
        out_specs=(
            P("tm", "rows", "cols", None),
            P(None, ("tm", "rows"), "cols"),
            P(None, ("tm", "rows"), "cols"),
        ),
        check_vma=False,
    )
```

```python
import functools

import jax
import jax.numpy as jnp
from jax import lax
from jax.experimental import pallas as pl
from jax.experimental.pallas import tpu as pltpu
from jax.sharding import PartitionSpec as P

MESH = pl.DeviceIdType.MESH
NT = (((1,), (1,)), ((), ()))


def kernel(
    dims,
    x_ref,
    c_ref,
    w1_ref,
    w2_ref,
    back_ref,
    acc,
    flat,
    edge,
    w1v,
    hid,
    gat,
    hal,
    sx,
    sg,
    sh,
    sa,
    imc,
    w1r,
    w2r,
    lt,
    pp,
    edges_out,
    edges_in,
    stage,
    landed,
    own_sem,
    w1_sem,
    w2_sem,
    blk_send,
    blk_recv,
    edge_send,
    edge_recv,
    hal_send,
    hal_recv,
    gh_send,
    gh_recv,
    rs_send,
    rs_recv,
):
    tmn, rn, zn, rows, cols, chunk, chunk_pad, slots = dims
    plane = tmn * rn
    height = rn * rows
    pitch = (height + 2) * cols
    cells = rows * cols
    frame_cells = height * cols
    span = tmn * pitch
    ochunk = 128 // zn
    tm, row, col = lax.axis_index("tm"), lax.axis_index("rows"), lax.axis_index("cols")
    me = tm * rn + row

    def place(index, z):
        return (index // rn, lax.rem(index, rn), z)

    has_low, has_high = col > 0, col < zn - 1

    barrier = pltpu.get_barrier_semaphore()

    def greet(index, z):
        pl.semaphore_signal(barrier, inc=1, device_id=place(index, z), device_id_type=MESH)

    for d in range(1, plane):
        greet(lax.rem(me + d, plane), col)

    for step in range(1, zn):
        greet(me, lax.rem(col + step, zn))

    blocks = (x_ref, c_ref)

    def keep(which):
        return pltpu.make_async_copy(blocks[which], gat.at[which, me], own_sem.at[which])

    def load_two(k):
        part = pl.ds(128 * k, 128)
        return pltpu.make_async_copy(w2_ref.at[part, :], w2r.at[:, part], w2_sem.at[k])

    load_one = pltpu.make_async_copy(w1_ref, w1v, w1_sem)
    keep(0).start()
    keep(1).start()
    load_one.start()
    for k in range(27):
        load_two(k).start()

    def blank(dst, lead):
        if lead:
            dst[:lead, :] = jnp.zeros((lead, 128), jnp.float32)
        for f in range(tmn):
            at = lead + f * pitch
            dst[at : at + cols, :] = jnp.zeros((cols, 128), jnp.float32)
            dst[at + pitch - cols : at + pitch, :] = jnp.zeros((cols, 128), jnp.float32)
        at = lead + span
        dst[at:, :] = jnp.zeros((dst.shape[0] - at, 128), jnp.float32)

    for e in range(3):
        blank(sx.at[e], 2 * pitch)
    for which in range(2):
        keep(which).wait()
        flat[...] = gat[which, me].astype(jnp.float32)
        for side in range(2):
            edge[side, which] = flat[pl.ds(side * (cols - 1), rows, stride=cols), :].astype(jnp.bfloat16)

    @pl.when(col == 0)
    def _():
        hal[me, 0] = jnp.zeros((2, rows, 128), jnp.bfloat16)

    @pl.when(col == zn - 1)
    def _():
        hal[me, 1] = jnp.zeros((2, rows, 128), jnp.bfloat16)

    pl.semaphore_wait(barrier, plane - 1 + zn - 1)

    def send_block(which, d):
        peer = lax.rem(me + d, plane)
        return pltpu.make_async_remote_copy(
            src_ref=gat.at[which, me],
            dst_ref=gat.at[which, me],
            send_sem=blk_send.at[which, d],
            recv_sem=blk_recv.at[which, me],
            device_id=place(peer, col),
            device_id_type=MESH,
        )

    def send_rim(side):
        return pltpu.make_async_remote_copy(
            src_ref=edge.at[side],
            dst_ref=hal.at[me, 1 - side],
            send_sem=edge_send.at[side],
            recv_sem=edge_recv.at[1 - side],
            device_id=place(me, col - 1 if side == 0 else col + 1),
            device_id_type=MESH,
        )

    def send_halo(d):
        return pltpu.make_async_remote_copy(
            src_ref=hal.at[me],
            dst_ref=hal.at[me],
            send_sem=hal_send.at[d],
            recv_sem=hal_recv.at[me],
            device_id=place(lax.rem(me + d, plane), col),
            device_id_type=MESH,
        )

    @pl.when(has_low)
    def _():
        send_rim(0).start()

    @pl.when(has_high)
    def _():
        send_rim(1).start()

    for d in range(1, plane):
        send_block(0, d).start()

    for e in range(3):
        blank(sg.at[e], 0)
    blank(sh.at[1], 0)
    for e in (0, 2):
        sh[e, span:, :] = jnp.zeros((sh.shape[1] - span, 128), jnp.float32)
    blank(sa, 2 * pitch)
    pp[27 * chunk_pad :, :] = jnp.zeros((pp.shape[0] - 27 * chunk_pad, 128), jnp.float32)

    def arrived(dst, sem, z):
        pltpu.make_async_remote_copy(
            src_ref=dst, dst_ref=dst, send_sem=sem, recv_sem=sem,
            device_id=place(me, z), device_id_type=MESH,
        ).wait_recv()

    @pl.when(has_low)
    def _():
        arrived(hal.at[me, 0], edge_recv.at[0], col - 1)

    @pl.when(has_high)
    def _():
        arrived(hal.at[me, 1], edge_recv.at[1], col + 1)

    for d in range(1, plane):
        send_halo(d).start()
    for d in range(1, plane):
        send_block(1, d).start()

    load_one.wait()
    for k in range(27):
        w1r[:, 128 * k : 128 * (k + 1)] = w1v[128 * k : 128 * (k + 1), :]

    def gather(which, dst, ahead):
        for m in range(plane):

            @pl.when(me != m)
            def _():
                arrived(gat.at[which, m], blk_recv.at[which, m], col)
                if which == 0:
                    arrived(hal.at[m], hal_recv.at[m], col)

            base = (m // rn + ahead) * pitch + (m % rn * rows + 1) * cols
            v = gat[which, m].astype(jnp.float32)
            dst[1, base : base + cells] = v
            dst[0, base + 1 : base + cells] = v[: cells - 1]
            dst[2, base : base + cells - 1] = v[1:]
            dst[0, pl.ds(base, rows, stride=cols), :] = hal[m, 0, which].astype(jnp.float32)
            dst[2, pl.ds(base + cols - 1, rows, stride=cols), :] = hal[m, 1, which].astype(jnp.float32)

    def past(src, base, count):
        for k in range(27):
            a, b, e = k // 9, k // 3 % 3, k % 3
            at = pl.multiple_of(base + a * pitch + b * cols, 8)
            imc[:count, 128 * k : 128 * (k + 1)] = src[e, pl.ds(at, count), :].astype(jnp.bfloat16)

    def future(src, base, count):
        for k in range(27):
            a, b, e = k // 9, k // 3 % 3, k % 3
            at = pl.multiple_of(base + (2 - a) * pitch + (2 - b) * cols, 8)
            imc[:count, 128 * k : 128 * (k + 1)] = src[2 - e, pl.ds(at, count), :].astype(jnp.bfloat16)

    group = slots * chunk_pad // zn
    taps = 27 * chunk_pad
    picked = jnp.where(
        (lax.broadcasted_iota(jnp.int32, (chunk_pad, 128), 1)
         == me * chunk + lax.broadcasted_iota(jnp.int32, (chunk_pad, 128), 0))
        & (lax.broadcasted_iota(jnp.int32, (chunk_pad, 128), 0) < chunk),
        1.0, 0.0,
    ).astype(jnp.bfloat16)

    def tall(src):
        return lax.dot_general(picked, src.astype(jnp.bfloat16), NT, preferred_element_type=jnp.float32)

    def send_piece(tensor, z):
        return pltpu.make_async_remote_copy(
            src_ref=stage.at[tensor, z],
            dst_ref=landed.at[tensor, col],
            send_sem=rs_send.at[tensor, z],
            recv_sem=rs_recv.at[tensor, col],
            device_id=place(me, z),
            device_id_type=MESH,
        )

    def scatter(tensor):
        for z in range(zn):
            stage[tensor, z] = jnp.concatenate(
                [pp[group * q : group * (q + 1), ochunk * z : ochunk * (z + 1)] for q in range(zn)],
                axis=1,
            ).astype(jnp.bfloat16)
        for z in range(zn):

            @pl.when(col != z)
            def _():
                send_piece(tensor, z).start()

    gather(0, sx, 2)

    def forward_step(t, carry):
        base = pl.multiple_of(t * pitch, 8)
        past(sx, base, frame_cells)
        hidden = jnp.dot(imc[:frame_cells, :], w1v[...], preferred_element_type=jnp.float32)
        hid[t] = hidden
        activation = (hidden * jax.nn.sigmoid(hidden)).astype(jnp.bfloat16)
        at = pl.multiple_of(base + cols + 2 * pitch, 8)
        sa[pl.ds(at, frame_cells), :] = activation.astype(jnp.float32)
        return carry

    lax.fori_loop(0, tmn, forward_step, 0)

    gather(1, sg, 0)
    at = tall(sa[...])
    for ab in range(9):
        off = ab // 3 * pitch + ab % 3 * cols
        lt[ab * chunk_pad : (ab + 1) * chunk_pad, :] = at[:, off : off + span].astype(jnp.bfloat16)
    for e in range(3):
        part = jnp.dot(
            lt[: 9 * chunk_pad, :], sg[2 - e, cols : cols + span, :].astype(jnp.bfloat16),
            preferred_element_type=jnp.float32,
        )
        for ab in range(9):
            k = 3 * ab + e
            pp[k * chunk_pad : (k + 1) * chunk_pad, :] = part[ab * chunk_pad : (ab + 1) * chunk_pad]
    scatter(1)

    for k in range(27):
        load_two(k).wait()

    def backward_step(t, carry):
        base = pl.multiple_of(t * pitch, 8)
        future(sg, base, frame_cells)
        grad_act = lax.dot_general(
            imc[:frame_cells, :], w2r[...], NT, preferred_element_type=jnp.float32
        )
        hidden = hid[t]
        squash = jax.nn.sigmoid(hidden)
        grad_hidden = (grad_act * squash * (1.0 + hidden * (1.0 - squash))).astype(jnp.bfloat16)
        at = pl.multiple_of(base + cols, 8)
        sh[1, pl.ds(at, frame_cells), :] = grad_hidden.astype(jnp.float32)
        return carry

    lax.fori_loop(0, tmn, backward_step, 0)

    lines = tmn * (height + 2)
    edges_out[0] = sh[1, pl.ds(0, lines, stride=cols), :].astype(jnp.bfloat16)
    edges_out[1] = sh[1, pl.ds(cols - 1, lines, stride=cols), :].astype(jnp.bfloat16)

    def send_edge(side):
        return pltpu.make_async_remote_copy(
            src_ref=edges_out.at[side],
            dst_ref=edges_in.at[1 - side],
            send_sem=gh_send.at[side],
            recv_sem=gh_recv.at[1 - side],
            device_id=place(me, col - 1 if side == 0 else col + 1),
            device_id_type=MESH,
        )

    @pl.when(has_low)
    def _():
        send_edge(0).start()

    @pl.when(has_high)
    def _():
        send_edge(1).start()

    for e in range(3):
        xt = tall(sx[e])
        for ab in range(9):
            off = ab // 3 * pitch + ab % 3 * cols
            k = 3 * ab + e
            lt[k * chunk_pad : (k + 1) * chunk_pad, :] = xt[:, off : off + span].astype(jnp.bfloat16)
    pp[:taps, :] = jnp.dot(
        lt[:taps, :], sh[1, cols : cols + span, :].astype(jnp.bfloat16),
        preferred_element_type=jnp.float32,
    )
    scatter(0)

    sh[0, 1 : span, :] = sh[1, : span - 1, :]
    sh[2, : span - 1, :] = sh[1, 1:span, :]
    nothing = jnp.zeros((lines, 128), jnp.float32)
    sh[0, pl.ds(0, lines, stride=cols), :] = nothing
    sh[2, pl.ds(cols - 1, lines, stride=cols), :] = nothing

    @pl.when(has_low)
    def _():
        arrived(edges_in.at[0], gh_recv.at[0], col - 1)
        sh[0, pl.ds(0, lines, stride=cols), :] = edges_in[0].astype(jnp.float32)

    @pl.when(has_high)
    def _():
        arrived(edges_in.at[1], gh_recv.at[1], col + 1)
        sh[2, pl.ds(cols - 1, lines, stride=cols), :] = edges_in[1].astype(jnp.float32)

    future(sh, pl.multiple_of(tm * pitch + row * cells, 8), cells)
    back_ref[...] = gat[1, me].astype(jnp.float32) + lax.dot_general(
        imc[:cells, :], w1r[...], NT, preferred_element_type=jnp.float32
    )

    for tensor in (1, 0):
        acc[tensor] = stage[tensor, col].astype(jnp.float32)
        for z in range(zn):

            @pl.when(col != z)
            def _():
                arrived(landed.at[tensor, z], rs_recv.at[tensor, z], z)
                acc[tensor] += landed[tensor, z].astype(jnp.float32)

    for which in range(2):
        for d in range(1, plane):
            send_block(which, d).wait_send()
        for z in range(zn):

            @pl.when(col != z)
            def _():
                send_piece(which, z).wait_send()

    for d in range(1, plane):
        send_halo(d).wait_send()

    @pl.when(has_low)
    def _():
        send_rim(0).wait_send()
        send_edge(0).wait_send()

    @pl.when(has_high)
    def _():
        send_rim(1).wait_send()
        send_edge(1).wait_send()


def finish(zn, chunk, chunk_pad, slots, back_ref, acc_ref, out_ref, one_ref, two_ref):
    ochunk = 128 // zn
    out_ref[...] = back_ref[...]
    for tensor, out in enumerate((one_ref, two_ref)):
        got = acc_ref[tensor]
        whole = jnp.concatenate(
            [got[:, ochunk * q : ochunk * (q + 1)] for q in range(zn)], axis=0
        ).reshape(slots, chunk_pad, ochunk)
        out[...] = whole[:27, :chunk, :]


def body(sizes, inputs, cotangent, weight_one, weight_two):
    tmn, rn, zn = sizes
    _, rows, cols, channels = inputs.shape
    plane = tmn * rn
    cells = rows * cols
    chunk = channels // plane
    chunk_pad = max(16, chunk)
    slots = 28
    pitch = (rn * rows + 2) * cols
    total = -(-((tmn + 2) * pitch + 2 * cols) // 128) * 128
    dims = (tmn, rn, zn, rows, cols, chunk, chunk_pad, slots)
    vmem = pl.BlockSpec(memory_space=pltpu.VMEM)
    bf, f32 = jnp.bfloat16, jnp.float32
    group = slots * chunk_pad // zn
    lines = tmn * (rn * rows + 2)
    frame_cells = rn * rows * cols
    dma = pltpu.SemaphoreType.DMA
    back, acc = pl.pallas_call(
        functools.partial(kernel, dims),
        out_shape=(
            jax.ShapeDtypeStruct((cells, channels), f32),
            jax.ShapeDtypeStruct((2, group, channels), f32),
        ),
        in_specs=[pl.BlockSpec(memory_space=pl.ANY)] * 4,
        out_specs=(vmem,) * 2,
        scratch_shapes=[
            pltpu.VMEM((cells, channels), f32),
            pltpu.VMEM((2, 2, rows, channels), bf),
            pltpu.VMEM((27 * channels, channels), bf),
            pltpu.VMEM((tmn, frame_cells, channels), f32),
            pltpu.VMEM((2, plane, cells, channels), bf),
            pltpu.VMEM((plane, 2, 2, rows, channels), bf),
            pltpu.VMEM((3, total, channels), f32),
            pltpu.VMEM((3, total, channels), f32),
            pltpu.VMEM((3, total, channels), f32),
            pltpu.VMEM((total, channels), f32),
            pltpu.VMEM((frame_cells, 27 * channels), bf),
            pltpu.VMEM((channels, 27 * channels), bf),
            pltpu.VMEM((channels, 27 * channels), bf),
            pltpu.VMEM((slots * chunk_pad, tmn * pitch), bf),
            pltpu.VMEM((slots * chunk_pad, channels), f32),
            pltpu.VMEM((2, lines, channels), bf),
            pltpu.VMEM((2, lines, channels), bf),
            pltpu.VMEM((2, zn, group, channels), bf),
            pltpu.VMEM((2, zn, group, channels), bf),
            dma((2,)),
            dma,
            dma((27,)),
            dma((2, plane)),
            dma((2, plane)),
            dma((2,)),
            dma((2,)),
            dma((plane,)),
            dma((plane,)),
            dma((2,)),
            dma((2,)),
            dma((2, zn)),
            dma((2, zn)),
        ],
        compiler_params=pltpu.CompilerParams(
            collective_id=0, has_side_effects=True, vmem_limit_bytes=60 * 1024 * 1024
        ),
    )(
        inputs.reshape(cells, channels),
        cotangent.reshape(cells, channels),
        weight_one.reshape(27 * channels, channels),
        weight_two.reshape(27 * channels, channels),
    )
    back, one, two = pl.pallas_call(
        functools.partial(finish, zn, chunk, chunk_pad, slots),
        out_shape=(
            jax.ShapeDtypeStruct((cells, channels), f32),
            jax.ShapeDtypeStruct((27, chunk, channels // zn), f32),
            jax.ShapeDtypeStruct((27, chunk, channels // zn), f32),
        ),
        in_specs=[vmem] * 2,
        out_specs=(vmem,) * 3,
    )(back, acc)
    return back.reshape(1, rows, cols, channels), one, two


def solution(mesh):
    sizes = (mesh.shape["tm"], mesh.shape["rows"], mesh.shape["cols"])
    placed = (P("tm", "rows", "cols", None), P("tm", "rows", "cols", None), P(), P())
    return jax.shard_map(
        functools.partial(body, sizes),
        mesh=mesh,
        in_specs=placed,
        out_specs=(
            P("tm", "rows", "cols", None),
            P(None, ("tm", "rows"), "cols"),
            P(None, ("tm", "rows"), "cols"),
        ),
        check_vma=False,
    )
```
